32 devices in a mesh: row: 16 (over z, x, core), col: 2 (over y).
Axes of the slice: x: 2, y: 2, z: 4, core: 2. Of those that a mesh axis runs over, the one named last changes fastest.
Arguments:
- tokens: bfloat16 [9232, 1024], P('row', 'col'), may hold values from -6 to 6
- gain_one: float32 [1024], P('col'), may hold values from 0.5 to 1.5
- shift_one: float32 [1024], P('col'), may hold values from -2.5 to 2.5
- qkv_weight: bfloat16 [3, 1024, 1024], P(None, 'row', 'col'), may hold values from -0.1875 to 0.1875
- qv_bias: float32 [2, 1024], P(None, 'col'), may hold values from -1.5 to 1.5
- proj_weight: bfloat16 [1024, 1024], P('col', 'row'), may hold values from -2.5 to 2.5
- proj_bias: float32 [1024], P('col'), may hold values from -2.5 to 2.5
- gain_two: float32 [1024], P('col'), may hold values from 0.5 to 1.5
- shift_two: float32 [1024], P('col'), may hold values from -2.5 to 2.5
- up_weight: bfloat16 [1024, 4096], P('row', 'col'), may hold values from -0.1875 to 0.1875
- up_bias: float32 [4096], P('col'), may hold values from -2.5 to 2.5
- down_weight: bfloat16 [4096, 1024], P('col', 'row'), may hold values from -0.09375 to 0.09375
- down_bias: float32 [1024], P('col'), may hold values from -2.5 to 2.5
- grad_out: bfloat16 [9232, 1024], P('row', 'col'), may hold values from -6 to 6
Outputs:
- output: bfloat16 [9232, 1024], P('row', 'col')
- grad_tokens: float32 [9232, 1024], P('row', 'col')
- grad_gain_one: float32 [1024], P('col')
- grad_shift_one: float32 [1024], P('col')
- grad_qkv_weight: float32 [3, 1024, 1024], P(None, 'row', 'col')
- grad_qv_bias: float32 [2, 1024], P(None, 'col')
- grad_proj_weight: float32 [1024, 1024], P('col', 'row')
- grad_proj_bias: float32 [1024], P('col')
- grad_gain_two: float32 [1024], P('col')
- grad_shift_two: float32 [1024], P('col')
- grad_up_weight: float32 [1024, 4096], P('row', 'col')
- grad_up_bias: float32 [4096], P('col')
- grad_down_weight: float32 [4096, 1024], P('col', 'row')
- grad_down_bias: float32 [1024], P('col')
The draws below stay inside these ranges and needn't reach their ends.
All inputs are finite; a program needn't handle non-finite values.
Results may differ from the reference program's by a relative error of at most 0.011.
Values may be sent and summed in bfloat16 or wider, within the bound.
A program may use at most 128 MiB of HBM per device.

```python
import math
import jax
import jax.numpy as jnp
from jax import lax

D = 1024
FF = 4096
HD = 64
SEQ = 577
IMG_DEV = 1
TOKENS = 9232
N_ROW = 16


def block_scale(key, dims, shards, low, high):
    gain, own = 1.0, jax.random.fold_in(key, 6)
    for dim, blocks in shards:
        heights = jnp.exp(jax.random.uniform(jax.random.fold_in(own, dim), (blocks,), jnp.float32, low / len(shards), high / len(shards)))
        gain = gain * jnp.repeat(heights, dims[dim] // blocks).reshape([-1 if axis == dim else 1 for axis in range(len(dims))])
    return gain


def centred(key, extent, width, limit, split=(), kind=jnp.bfloat16):
    values = jax.random.normal(key, extent, jnp.float32) * width
    if len(split) > 0:
        values = block_scale(key, extent, split, -0.22, 0.18) * values
    return jnp.clip(values, min=-limit, max=limit).astype(kind)


def setup_inputs(seed: int = 0) -> dict:
    key_of = jax.random.split(jax.random.key(seed), 15)
    tokens = centred(key_of[0], (TOKENS, D), 1.0, 6.0, ((0, 16), (1, 2)))
    gain_one = jnp.clip(1.0 + 0.1 * jax.random.normal(key_of[1], (D,), jnp.float32), 0.5, 1.5)
    shift_one = centred(key_of[2], (D,), 0.3, 2.5, ((0, 2),), jnp.float32)
    qkv_weight = centred(key_of[3], (3, D, D), D ** -0.5, 0.1875, ((1, 16), (2, 2)))
    qv_bias = centred(key_of[4], (2, D), 0.1, 1.5, ((1, 2),), jnp.float32)
    proj_weight = centred(key_of[5], (D, D), (3 * D // SEQ) ** -0.5, 2.5, ((0, 2), (1, 16)))
    proj_bias = centred(key_of[6], (D,), 0.3, 2.5, ((0, 2),), jnp.float32)
    gain_two = jnp.clip(1.0 + 0.1 * jax.random.normal(key_of[7], (D,), jnp.float32), 0.5, 1.5)
    shift_two = centred(key_of[8], (D,), 0.3, 2.5, ((0, 2),), jnp.float32)
    up_weight = centred(key_of[9], (D, FF), D ** -0.5, 0.1875, ((0, 16), (1, 2)))
    up_bias = centred(key_of[10], (FF,), 0.5, 2.5, ((0, 2),), jnp.float32)
    down_weight = centred(key_of[11], (FF, D), FF ** -0.5, 0.09375, ((0, 2), (1, 16)))
    down_bias = centred(key_of[12], (D,), 0.3, 2.5, ((0, 2),), jnp.float32)
    grad_out = centred(key_of[13], (TOKENS, D), 1.0, 6.0, ((0, 16), (1, 2)))
    return dict(tokens=tokens, gain_one=gain_one, shift_one=shift_one, qkv_weight=qkv_weight, qv_bias=qv_bias, proj_weight=proj_weight, proj_bias=proj_bias, gain_two=gain_two, shift_two=shift_two, up_weight=up_weight, up_bias=up_bias, down_weight=down_weight, down_bias=down_bias, grad_out=grad_out)


epsilon = 1e-06
highest = lax.Precision.HIGHEST

@jax.custom_vjp
def low(v):
    return lax.optimization_barrier(v.astype(jnp.bfloat16)).astype(jnp.float32)

@jax.custom_vjp
def low_back(v):
    return v

def low_keep(v):
    return (low(v), None)

def low_pass(kept, grad):
    return (grad,)

def back_keep(v):
    return (v, None)

def back_low(kept, grad):
    return (low(grad),)
low.defvjp(low_keep, low_pass)
low_back.defvjp(back_keep, back_low)

def normalize(values, gain_value, shift_value):
    center = lax.optimization_barrier(jnp.mean(values, axis=-1, keepdims=True))
    spread = lax.optimization_barrier(jnp.mean(values * values, axis=-1, keepdims=True)) - center * center
    return (values - center) * lax.rsqrt(spread + epsilon) * gain_value + shift_value

def block_forward(inputs, gain_one, shift_one, qkv_weight, qv_bias, proj_weight, proj_bias, gain_two, shift_two, up_weight, up_bias, down_weight, down_bias):
    image_count = inputs.shape[0] // SEQ
    head_count = D // HD
    score_scale = HD ** (-0.5)

    def to_images(values):
        return values.reshape(image_count, SEQ, head_count, HD)
    input_one = low(normalize(inputs, gain_one, shift_one))
    projected = jnp.einsum('td,jde->jte', input_one, qkv_weight, precision=highest)
    query_rows = low(low_back(projected[0] + qv_bias[0]))
    key_rows = low(low_back(projected[1]))
    value_rows = low(low_back(projected[2] + qv_bias[1]))
    scores = low_back(score_scale * jnp.einsum('gqhe,gkhe->ghqk', to_images(query_rows), to_images(key_rows), precision=highest))
    weights_low = low(jax.nn.softmax(scores, axis=-1))
    mixed_heads = jnp.einsum('ghqk,gkhe->gqhe', weights_low, to_images(value_rows), precision=highest)
    mixed_heads = low(low_back(mixed_heads.reshape(inputs.shape[0], D)))
    branch_out = low_back(jnp.dot(mixed_heads, proj_weight, precision=highest) + proj_bias)
    hidden = inputs + branch_out
    input_two = low(normalize(hidden, gain_two, shift_two))
    up_value = low_back(jnp.dot(input_two, up_weight, precision=highest) + up_bias)
    activated = low(jax.nn.gelu(up_value, approximate=False))
    down_value = low_back(jnp.dot(activated, down_weight, precision=highest) + down_bias)
    return hidden + down_value

def reference(tokens, gain_one, shift_one, qkv_weight, qv_bias, proj_weight, proj_bias, gain_two, shift_two, up_weight, up_bias, down_weight, down_bias, grad_out):
    params = tuple((item.astype(jnp.float32) for item in (gain_one, shift_one, qkv_weight, qv_bias, proj_weight, proj_bias, gain_two, shift_two, up_weight, up_bias, down_weight, down_bias)))
    group_rows = math.gcd(IMG_DEV * N_ROW, 4) * SEQ
    group_count = tokens.shape[0] // group_rows
    inputs = tokens.astype(jnp.float32).reshape(group_count, group_rows, D)
    upstream = grad_out.astype(jnp.float32).reshape(group_count, group_rows, D)
    zeros = tuple((jnp.zeros_like(item) for item in params))

    def one_group(totals, pair):
        result, pull = jax.vjp(block_forward, pair[0], *params)
        grads = pull(pair[1])
        totals = tuple((first + second for first, second in zip(totals, grads[1:])))
        return (totals, (result.astype(jnp.bfloat16), grads[0]))
    totals, (results, input_grads) = lax.scan(one_group, zeros, (inputs, upstream))
    return (results.reshape(-1, D), input_grads.reshape(-1, D), totals[0], totals[1], totals[2], totals[3], totals[4], totals[5], totals[6], totals[7], totals[8], totals[9], totals[10], totals[11])
```

```python
from functools import partial

import jax
import jax.numpy as jnp
from jax import lax
from jax.sharding import PartitionSpec as P

D = 1024
HD = 64
SEQ = 577


epsilon = 1e-06


def row_totals(first_term, second_term):
    return lax.psum((jnp.sum(first_term, axis=1), jnp.sum(second_term, axis=1)), "col")


def norm_forward(values, gain_value, shift_value, feature_width):
    row_total, squares = row_totals(values, values * values)
    center = row_total / feature_width
    spread = squares / feature_width - center * center
    inverse = lax.rsqrt(spread + epsilon)
    normed = (values - center[:, None]) * inverse[:, None]
    return (normed, inverse, normed * gain_value + shift_value)


def norm_backward(grad_in, normed, inverse, gain_value, feature_width):
    scaled = grad_in * gain_value
    row_total, cross_sum = row_totals(scaled, scaled * normed)
    return inverse[:, None] * (
        scaled - row_total[:, None] / feature_width - normed * (cross_sum[:, None] / feature_width)
    )


def column_ring(shift):
    count = lax.axis_size("col")
    return [(i, (i + shift) % count) for i in range(count)]


def spread(values):
    count, here = lax.axis_size("col"), lax.axis_index("col")
    width = values.shape[1]
    out = jnp.zeros((values.shape[0], width * count), values.dtype)
    out = lax.dynamic_update_slice(out, values, (0, here * width))
    for shift in range(1, count):
        got = lax.ppermute(values, "col", column_ring(shift))
        out = lax.dynamic_update_slice(out, got, (0, ((here - shift) % count) * width))
    return out


def collect(term):
    count, here = lax.axis_size("col"), lax.axis_index("col")
    width = term.shape[1] // count
    total = lax.dynamic_slice_in_dim(term, here * width, width, 1)
    for shift in range(1, count):
        block = lax.dynamic_slice_in_dim(term, ((here + shift) % count) * width, width, 1)
        got = lax.ppermute(block.astype(jnp.bfloat16), "col", column_ring(shift))
        total = total + got.astype(jnp.float32)
    return total


def gather_rows(block):
    return lax.all_gather(block, "row", axis=0, tiled=True)


def scatter_rows(term):
    count = lax.axis_size("row")
    chips = count // 2
    pairs = [[i, i + 1] for i in range(0, count, 2)]
    rings = [list(range(0, count, 2)), list(range(1, count, 2))]
    rows, width = term.shape
    term = term.reshape(chips, 2, rows // count, width).swapaxes(0, 1)
    got = lax.all_to_all(term.astype(jnp.bfloat16), "row", 0, 0, axis_index_groups=pairs)
    half = jnp.sum(got.astype(jnp.float32), axis=0).astype(jnp.bfloat16)
    got = lax.all_to_all(half, "row", 0, 0, axis_index_groups=rings)
    return jnp.sum(got.astype(jnp.float32), axis=0)


def sum_small(parts):
    flat = jnp.concatenate([part.reshape(-1) for part in parts])
    flat = jnp.sum(lax.all_gather(flat, "row", axis=0), axis=0)
    outs, start = [], 0
    for part in parts:
        outs.append(flat[start : start + part.size].reshape(part.shape))
        start += part.size
    return outs


def attend(item_tuple, score_scale):
    query_part, key_part, value_part = item_tuple
    scores = score_scale * jnp.einsum(
        "qhe,khe->hqk", query_part, key_part, preferred_element_type=jnp.float32
    )
    largest = jnp.max(scores, axis=-1, keepdims=True)
    shifted = jnp.exp(scores - largest)
    row_total = jnp.sum(shifted, axis=-1, keepdims=True)
    weights_low = (shifted / row_total).astype(jnp.bfloat16)
    mixed_part = jnp.einsum(
        "hqk,khe->qhe", weights_low, value_part, preferred_element_type=jnp.float32
    )
    return (mixed_part.astype(jnp.bfloat16), (largest + jnp.log(row_total))[..., 0])


def attend_back(item_tuple, score_scale):
    query_part, key_part, value_part, grad_part, log_total = item_tuple
    scores = score_scale * jnp.einsum(
        "qhe,khe->hqk", query_part, key_part, preferred_element_type=jnp.float32
    )
    weights = jnp.exp(scores - log_total[..., None])
    weights_low = weights.astype(jnp.bfloat16)
    grad_value = jnp.einsum(
        "hqk,qhe->khe", weights_low, grad_part, preferred_element_type=jnp.float32
    )
    grad_weights = jnp.einsum(
        "qhe,khe->hqk", grad_part, value_part, preferred_element_type=jnp.float32
    )
    grad_scores = (
        weights * (grad_weights - jnp.sum(weights * grad_weights, axis=-1, keepdims=True))
    ).astype(jnp.bfloat16)
    grad_query = score_scale * jnp.einsum(
        "hqk,khe->qhe", grad_scores, key_part, preferred_element_type=jnp.float32
    )
    grad_key = score_scale * jnp.einsum(
        "hqk,qhe->khe", grad_scores, query_part, preferred_element_type=jnp.float32
    )
    return (grad_query, grad_key, grad_value)


def on_device(
    tokens,
    gain_one,
    shift_one,
    qkv_weight,
    qv_bias,
    proj_weight,
    proj_bias,
    gain_two,
    shift_two,
    up_weight,
    up_bias,
    down_weight,
    down_bias,
    grad_out,
):
    row_count = tokens.shape[0]
    local_width = tokens.shape[1]
    head_count = local_width // HD
    image_count = row_count // SEQ
    score_scale = HD ** (-0.5)

    def to_images(values):
        return values.reshape(image_count, SEQ, head_count, HD)

    qkv_full, proj_full, up_full, down_full = (
        gather_rows(qkv_weight.swapaxes(0, 1).reshape(-1, 3 * local_width)),
        gather_rows(proj_weight.T),
        gather_rows(up_weight),
        gather_rows(down_weight.T),
    )
    x_value = tokens.astype(jnp.float32)
    normed_one, inverse_one, pre_one = norm_forward(x_value, gain_one, shift_one, D)
    input_one = spread(pre_one.astype(jnp.bfloat16))
    projected = jnp.dot(input_one, qkv_full, preferred_element_type=jnp.float32)
    query_rows = (projected[:, :local_width] + qv_bias[0]).astype(jnp.bfloat16)
    key_rows = projected[:, local_width : 2 * local_width].astype(jnp.bfloat16)
    value_rows = (projected[:, 2 * local_width :] + qv_bias[1]).astype(jnp.bfloat16)
    mixed_heads, log_total = lax.map(
        partial(attend, score_scale=score_scale),
        (to_images(query_rows), to_images(key_rows), to_images(value_rows)),
    )
    mixed_heads = mixed_heads.reshape(row_count, local_width)
    branch_out = (
        collect(jnp.einsum("te,de->td", mixed_heads, proj_full, preferred_element_type=jnp.float32))
        + proj_bias
    )
    hidden = x_value + branch_out
    normed_two, inverse_two, pre_two = norm_forward(hidden, gain_two, shift_two, D)
    input_two = spread(pre_two.astype(jnp.bfloat16))
    up_value = jnp.dot(input_two, up_full, preferred_element_type=jnp.float32) + up_bias
    activated = jax.nn.gelu(up_value, approximate=False).astype(jnp.bfloat16)
    down_value = (
        collect(jnp.einsum("tf,df->td", activated, down_full, preferred_element_type=jnp.float32)) + down_bias
    )
    output = (hidden + down_value).astype(jnp.bfloat16)
    upstream = grad_out.astype(jnp.float32)
    grad_down_bias = jnp.sum(upstream, axis=0)
    down_grads_full = spread(grad_out)
    w_down_term = jnp.einsum(
        "td,tf->df", down_grads_full, activated, preferred_element_type=jnp.float32
    )
    grad_down_weight = scatter_rows(w_down_term).T
    grad_activated = jnp.einsum(
        "td,df->tf", down_grads_full, down_full, preferred_element_type=jnp.float32
    )
    unused_value, gelu_pull = jax.vjp(
        lambda inner_value: jax.nn.gelu(inner_value, approximate=False), up_value
    )
    grad_up = gelu_pull(grad_activated)[0].astype(jnp.bfloat16)
    grad_up_bias = jnp.sum(grad_up, axis=0, dtype=jnp.float32)
    w_up_term = jnp.einsum("td,tf->df", input_two, grad_up, preferred_element_type=jnp.float32)
    grad_up_weight = scatter_rows(w_up_term)
    grad_input_two = collect(
        jnp.einsum("tf,df->td", grad_up, up_full, preferred_element_type=jnp.float32)
    )
    grad_gain_two = jnp.sum(grad_input_two * normed_two, axis=0)
    grad_shift_two = jnp.sum(grad_input_two, axis=0)
    grad_hidden = upstream + norm_backward(grad_input_two, normed_two, inverse_two, gain_two, D)
    grad_branch = grad_hidden.astype(jnp.bfloat16)
    grad_proj_bias = jnp.sum(grad_branch, axis=0, dtype=jnp.float32)
    branch_grads_full = spread(grad_branch)
    w_proj_term = jnp.einsum(
        "td,te->de", branch_grads_full, mixed_heads, preferred_element_type=jnp.float32
    )
    grad_proj_weight = scatter_rows(w_proj_term).T
    grad_mixed = jnp.einsum(
        "td,de->te", branch_grads_full, proj_full, preferred_element_type=jnp.float32
    ).astype(jnp.bfloat16)
    grad_query, grad_key, grad_value = lax.map(
        partial(attend_back, score_scale=score_scale),
        (
            to_images(query_rows),
            to_images(key_rows),
            to_images(value_rows),
            to_images(grad_mixed),
            log_total,
        ),
    )
    grad_stack = jnp.concatenate(
        [
            grad_query.reshape(row_count, local_width),
            grad_key.reshape(row_count, local_width),
            grad_value.reshape(row_count, local_width),
        ],
        axis=1,
    ).astype(jnp.bfloat16)
    stack_sums = jnp.sum(grad_stack, axis=0, dtype=jnp.float32)
    grad_qv_bias = jnp.stack([stack_sums[:local_width], stack_sums[2 * local_width :]])
    w_qkv_term = jnp.einsum(
        "td,te->de", input_one, grad_stack, preferred_element_type=jnp.float32
    )
    grad_qkv_weight = scatter_rows(w_qkv_term).reshape(-1, 3, local_width).swapaxes(0, 1)
    grad_input_one = collect(
        jnp.einsum("te,de->td", grad_stack, qkv_full, preferred_element_type=jnp.float32)
    )
    grad_gain_one = jnp.sum(grad_input_one * normed_one, axis=0)
    grad_shift_one = jnp.sum(grad_input_one, axis=0)
    grad_tokens = grad_hidden + norm_backward(grad_input_one, normed_one, inverse_one, gain_one, D)
    small_sums = sum_small(
        (
            grad_gain_one,
            grad_shift_one,
            grad_qv_bias,
            grad_proj_bias,
            grad_gain_two,
            grad_shift_two,
            grad_up_bias,
            grad_down_bias,
        )
    )
    return (
        output,
        grad_tokens,
        small_sums[0],
        small_sums[1],
        grad_qkv_weight,
        small_sums[2],
        grad_proj_weight,
        small_sums[3],
        small_sums[4],
        small_sums[5],
        grad_up_weight,
        small_sums[6],
        grad_down_weight,
        small_sums[7],
    )


def solution(mesh):
    return jax.shard_map(
        on_device,
        mesh=mesh,
        in_specs=(
            P("row", "col"),
            P("col"),
            P("col"),
            P(None, "row", "col"),
            P(None, "col"),
            P("col", "row"),
            P("col"),
            P("col"),
            P("col"),
            P("row", "col"),
            P("col"),
            P("col", "row"),
            P("col"),
            P("row", "col"),
        ),
        out_specs=(
            P("row", "col"),
            P("row", "col"),
            P("col"),
            P("col"),
            P(None, "row", "col"),
            P(None, "col"),
            P("col", "row"),
            P("col"),
            P("col"),
            P("col"),
            P("row", "col"),
            P("col"),
            P("col", "row"),
            P("col"),
        ),
        check_vma=False,
    )
```

```python
from functools import partial

import jax
import jax.numpy as jnp
from jax import lax
from jax.sharding import PartitionSpec as P

D = 1024
HD = 64
SEQ = 577


epsilon = 1e-06


def row_totals(first_term, second_term):
    sums = jnp.stack([jnp.sum(first_term, axis=1), jnp.sum(second_term, axis=1)])
    total = sums
    for shift in range(1, lax.axis_size("col")):
        total = total + lax.ppermute(sums, "col", column_ring(shift))
    return total[0], total[1]


def norm_forward(values, gain_value, shift_value, feature_width):
    row_total, squares = row_totals(values, values * values)
    center = row_total / feature_width
    spread = squares / feature_width - center * center
    inverse = lax.rsqrt(spread + epsilon)
    normed = (values - center[:, None]) * inverse[:, None]
    return (normed, inverse, normed * gain_value + shift_value)


def norm_backward(grad_in, normed, inverse, gain_value, feature_width):
    scaled = grad_in * gain_value
    row_total, cross_sum = row_totals(scaled, scaled * normed)
    return inverse[:, None] * (
        scaled - row_total[:, None] / feature_width - normed * (cross_sum[:, None] / feature_width)
    )


def column_ring(shift):
    count = lax.axis_size("col")
    return [(i, (i + shift) % count) for i in range(count)]


def spread(values):
    count, here = lax.axis_size("col"), lax.axis_index("col")
    width = values.shape[1]
    out = jnp.zeros((values.shape[0], width * count), values.dtype)
    out = lax.dynamic_update_slice(out, values, (0, here * width))
    for shift in range(1, count):
        got = lax.ppermute(values, "col", column_ring(shift))
        out = lax.dynamic_update_slice(out, got, (0, ((here - shift) % count) * width))
    return out


def collect(term):
    count, here = lax.axis_size("col"), lax.axis_index("col")
    width = term.shape[1] // count
    total = lax.dynamic_slice_in_dim(term, here * width, width, 1)
    for shift in range(1, count):
        block = lax.dynamic_slice_in_dim(term, ((here + shift) % count) * width, width, 1)
        got = lax.ppermute(block.astype(jnp.bfloat16), "col", column_ring(shift))
        total = total + got.astype(jnp.float32)
    return total


def gather_rows(block):
    return lax.all_gather(block, "row", axis=0, tiled=True)


def halve(term):
    count, core = lax.axis_size("row"), lax.axis_index("row") % 2
    rows, width = term.shape
    term = term.reshape(count // 2, 2, rows // count, width)
    mine = lax.dynamic_index_in_dim(term, core, 1, keepdims=False)
    other = lax.dynamic_index_in_dim(term, 1 - core, 1, keepdims=False)
    got = lax.ppermute(other.astype(jnp.bfloat16), "row", [(i, i ^ 1) for i in range(count)])
    return (mine + got.astype(jnp.float32)).astype(jnp.bfloat16)


def scatter_rows(half):
    count = lax.axis_size("row")
    rings = [list(range(0, count, 2)), list(range(1, count, 2))]
    got = lax.all_to_all(half, "row", 0, 0, axis_index_groups=rings)
    return jnp.sum(got.astype(jnp.float32), axis=0)


def sum_small(parts):
    flat = jnp.concatenate([part.reshape(-1) for part in parts])
    count, step = lax.axis_size("row"), 1
    while step < count:
        flat = flat + lax.ppermute(flat, "row", [(i, i ^ step) for i in range(count)])
        step *= 2
    outs, start = [], 0
    for part in parts:
        outs.append(flat[start : start + part.size].reshape(part.shape))
        start += part.size
    return outs


def attend(item_tuple, score_scale):
    query_part, key_part, value_part = item_tuple
    scores = score_scale * jnp.einsum(
        "qhe,khe->hqk", query_part, key_part, preferred_element_type=jnp.float32
    )
    largest = jnp.max(scores, axis=-1, keepdims=True)
    shifted = jnp.exp(scores - largest)
    row_total = jnp.sum(shifted, axis=-1, keepdims=True)
    weights_low = (shifted / row_total).astype(jnp.bfloat16)
    mixed_part = jnp.einsum(
        "hqk,khe->qhe", weights_low, value_part, preferred_element_type=jnp.float32
    )
    return (mixed_part.astype(jnp.bfloat16), (largest + jnp.log(row_total))[..., 0])


def attend_back(item_tuple, score_scale):
    query_part, key_part, value_part, grad_part, log_total = item_tuple
    scores = score_scale * jnp.einsum(
        "qhe,khe->hqk", query_part, key_part, preferred_element_type=jnp.float32
    )
    weights = jnp.exp(scores - log_total[..., None])
    weights_low = weights.astype(jnp.bfloat16)
    grad_value = jnp.einsum(
        "hqk,qhe->khe", weights_low, grad_part, preferred_element_type=jnp.float32
    )
    grad_weights = jnp.einsum(
        "qhe,khe->hqk", grad_part, value_part, preferred_element_type=jnp.float32
    )
    grad_scores = (
        weights * (grad_weights - jnp.sum(weights * grad_weights, axis=-1, keepdims=True))
    ).astype(jnp.bfloat16)
    grad_query = score_scale * jnp.einsum(
        "hqk,khe->qhe", grad_scores, key_part, preferred_element_type=jnp.float32
    )
    grad_key = score_scale * jnp.einsum(
        "hqk,qhe->khe", grad_scores, query_part, preferred_element_type=jnp.float32
    )
    return (grad_query, grad_key, grad_value)


def on_device(
    tokens,
    gain_one,
    shift_one,
    qkv_weight,
    qv_bias,
    proj_weight,
    proj_bias,
    gain_two,
    shift_two,
    up_weight,
    up_bias,
    down_weight,
    down_bias,
    grad_out,
):
    row_count = tokens.shape[0]
    local_width = tokens.shape[1]
    head_count = local_width // HD
    image_count = row_count // SEQ
    score_scale = HD ** (-0.5)

    def to_images(values):
        return values.reshape(image_count, SEQ, head_count, HD)

    hidden_width = up_weight.shape[1]
    first_full = gather_rows(
        jnp.concatenate(
            [qkv_weight[0], qkv_weight[1], qkv_weight[2], proj_weight.T], axis=1
        )
    )
    second_full = gather_rows(jnp.concatenate([up_weight, down_weight.T], axis=1))
    qkv_full, proj_full = first_full[:, : 3 * local_width], first_full[:, 3 * local_width :]
    up_full, down_full = second_full[:, :hidden_width], second_full[:, hidden_width:]
    x_value = tokens.astype(jnp.float32)
    normed_one, inverse_one, pre_one = norm_forward(x_value, gain_one, shift_one, D)
    input_one = spread(pre_one.astype(jnp.bfloat16))
    projected = jnp.dot(input_one, qkv_full, preferred_element_type=jnp.float32)
    query_rows = (projected[:, :local_width] + qv_bias[0]).astype(jnp.bfloat16)
    key_rows = projected[:, local_width : 2 * local_width].astype(jnp.bfloat16)
    value_rows = (projected[:, 2 * local_width :] + qv_bias[1]).astype(jnp.bfloat16)
    mixed_heads, log_total = lax.map(
        partial(attend, score_scale=score_scale),
        (to_images(query_rows), to_images(key_rows), to_images(value_rows)),
    )
    mixed_heads = mixed_heads.reshape(row_count, local_width)
    branch_out = (
        collect(jnp.einsum("te,de->td", mixed_heads, proj_full, preferred_element_type=jnp.float32))
        + proj_bias
    )
    hidden = x_value + branch_out
    normed_two, inverse_two, pre_two = norm_forward(hidden, gain_two, shift_two, D)
    input_two = spread(pre_two.astype(jnp.bfloat16))
    up_value = jnp.dot(input_two, up_full, preferred_element_type=jnp.float32) + up_bias
    activated = jax.nn.gelu(up_value, approximate=False).astype(jnp.bfloat16)
    down_value = (
        collect(jnp.einsum("tf,df->td", activated, down_full, preferred_element_type=jnp.float32)) + down_bias
    )
    output = (hidden + down_value).astype(jnp.bfloat16)
    upstream = grad_out.astype(jnp.float32)
    grad_down_bias = jnp.sum(upstream, axis=0)
    down_grads_full = spread(grad_out)
    w_down_term = jnp.einsum(
        "td,tf->df", down_grads_full, activated, preferred_element_type=jnp.float32
    )
    down_half = halve(w_down_term)
    grad_activated = jnp.einsum(
        "td,df->tf", down_grads_full, down_full, preferred_element_type=jnp.float32
    )
    unused_value, gelu_pull = jax.vjp(
        lambda inner_value: jax.nn.gelu(inner_value, approximate=False), up_value
    )
    grad_up = gelu_pull(grad_activated)[0].astype(jnp.bfloat16)
    down_half, grad_up = lax.optimization_barrier((down_half, grad_up))
    grad_down_weight = scatter_rows(down_half).T
    grad_up_bias = jnp.sum(grad_up, axis=0, dtype=jnp.float32)
    w_up_term = jnp.einsum("td,tf->df", input_two, grad_up, preferred_element_type=jnp.float32)
    up_half = halve(w_up_term)
    grad_input_two = collect(
        jnp.einsum("tf,df->td", grad_up, up_full, preferred_element_type=jnp.float32)
    )
    grad_gain_two = jnp.sum(grad_input_two * normed_two, axis=0)
    grad_shift_two = jnp.sum(grad_input_two, axis=0)
    grad_hidden = upstream + norm_backward(grad_input_two, normed_two, inverse_two, gain_two, D)
    grad_branch = grad_hidden.astype(jnp.bfloat16)
    up_half, grad_branch = lax.optimization_barrier((up_half, grad_branch))
    grad_up_weight = scatter_rows(up_half)
    grad_proj_bias = jnp.sum(grad_branch, axis=0, dtype=jnp.float32)
    branch_grads_full = spread(grad_branch)
    w_proj_term = jnp.einsum(
        "td,te->de", branch_grads_full, mixed_heads, preferred_element_type=jnp.float32
    )
    proj_half = halve(w_proj_term)
    grad_mixed = jnp.einsum(
        "td,de->te", branch_grads_full, proj_full, preferred_element_type=jnp.float32
    ).astype(jnp.bfloat16)
    proj_half, grad_mixed = lax.optimization_barrier((proj_half, grad_mixed))
    grad_proj_weight = scatter_rows(proj_half).T
    grad_query, grad_key, grad_value = lax.map(
        partial(attend_back, score_scale=score_scale),
        (
            to_images(query_rows),
            to_images(key_rows),
            to_images(value_rows),
            to_images(grad_mixed),
            log_total,
        ),
    )
    grad_stack = jnp.concatenate(
        [
            grad_query.reshape(row_count, local_width),
            grad_key.reshape(row_count, local_width),
            grad_value.reshape(row_count, local_width),
        ],
        axis=1,
    ).astype(jnp.bfloat16)
    stack_sums = jnp.sum(grad_stack, axis=0, dtype=jnp.float32)
    grad_qv_bias = jnp.stack([stack_sums[:local_width], stack_sums[2 * local_width :]])
    w_qkv_term = jnp.einsum(
        "td,te->de", input_one, grad_stack, preferred_element_type=jnp.float32
    )
    grad_qkv_weight = scatter_rows(halve(w_qkv_term)).reshape(-1, 3, local_width).swapaxes(0, 1)
    grad_input_one = collect(
        jnp.einsum("te,de->td", grad_stack, qkv_full, preferred_element_type=jnp.float32)
    )
    grad_gain_one = jnp.sum(grad_input_one * normed_one, axis=0)
    grad_shift_one = jnp.sum(grad_input_one, axis=0)
    grad_tokens = grad_hidden + norm_backward(grad_input_one, normed_one, inverse_one, gain_one, D)
    small_sums = sum_small(
        (
            grad_gain_one,
            grad_shift_one,
            grad_qv_bias,
            grad_proj_bias,
            grad_gain_two,
            grad_shift_two,
            grad_up_bias,
            grad_down_bias,
        )
    )
    return (
        output,
        grad_tokens,
        small_sums[0],
        small_sums[1],
        grad_qkv_weight,
        small_sums[2],
        grad_proj_weight,
        small_sums[3],
        small_sums[4],
        small_sums[5],
        grad_up_weight,
        small_sums[6],
        grad_down_weight,
        small_sums[7],
    )


def solution(mesh):
    return jax.shard_map(
        on_device,
        mesh=mesh,
        in_specs=(
            P("row", "col"),
            P("col"),
            P("col"),
            P(None, "row", "col"),
            P(None, "col"),
            P("col", "row"),
            P("col"),
            P("col"),
            P("col"),
            P("row", "col"),
            P("col"),
            P("col", "row"),
            P("col"),
            P("row", "col"),
        ),
        out_specs=(
            P("row", "col"),
            P("row", "col"),
            P("col"),
            P("col"),
            P(None, "row", "col"),
            P(None, "col"),
            P("col", "row"),
            P("col"),
            P("col"),
            P("col"),
            P("row", "col"),
            P("col"),
            P("col", "row"),
            P("col"),
        ),
        check_vma=False,
    )
```
